256 devices in a mesh: param: 64 (over z, x, core), ex: 4 (over y).
Axes of the slice: x: 4, y: 4, z: 8, core: 2. Of those that a mesh axis runs over, the one named last changes fastest.
Arguments:
- gradients: bfloat16 [512, 524288], P('ex', 'param'), may hold values from -60 to 60
- projection_seed: int32 [1], replicated, may hold values from 0 to 1048575
- target_features: bfloat16 [512, 4096], replicated, may hold values from -0.09375 to 0.09375
Outputs:
- scores: float32 [512, 512], P('param', 'ex')
The draws below stay inside these ranges and needn't reach their ends.
All inputs are finite; a program needn't handle non-finite values.
Results may differ from the reference program's by a relative error of at most 0.011.
Values may be sent and summed in bfloat16 or wider, within the bound.
No kernel may reach another device: no remote copies, remote signals or barrier semaphores. Data moves between devices by JAX's collectives and lax.ppermute only.
A program may use at most 64 MiB of HBM per device.

```python
import math
import jax
import jax.numpy as jnp
from jax import lax

FEATS = 4096
BLOCK = 128
STEPS = 10
COORD_DEV = 8192
TARGET_ROWS = 512
COORDS = 524288
EXAMPLES = 512
N_PARAM = 64


def draw_gradients(key, part):
    key_noise, key_rows, key_cols = jax.random.split(key, 3)
    noise = jax.random.truncated_normal(key_noise, -5.0, 5.0, (EXAMPLES, COORDS), jnp.float32)
    col_scale = jnp.exp(jax.random.uniform(key_cols, (1, COORDS), jnp.float32, jnp.log(0.5), jnp.log(2.0)))
    row_scale = jnp.exp(jax.random.uniform(key_rows, (EXAMPLES, 1), jnp.float32, jnp.log(0.3), jnp.log(3.0)))
    return (noise * row_scale * col_scale).astype(jnp.bfloat16)


def gaussian(own_key, extent, spread, most, kind=jnp.bfloat16):
    return jnp.clip(spread * jax.random.normal(own_key, extent, jnp.float32), -most, most).astype(kind)


def setup_inputs(seed: int = 0) -> dict:
    arg_keys = jax.random.split(jax.random.key(seed), 4)
    return {
        "gradients": draw_gradients(jax.random.fold_in(arg_keys[3], 71), 0),
        "projection_seed": jax.random.randint(arg_keys[1], (1,), 0, 1048576).astype(jnp.int32),
        "target_features": gaussian(arg_keys[2], (TARGET_ROWS, FEATS), FEATS ** -0.5, 0.09375),
    }


DAMPING = 0.001

def hashed(seed_value, row_start, row_count, col_start, col_count, total_coords):
    row_index = (row_start + lax.iota(jnp.int32, row_count)).reshape(row_count, 1)
    col_index = (col_start + lax.iota(jnp.int32, col_count)).reshape(1, col_count)
    mixed = row_index * 73856093 ^ col_index * 19349663 ^ seed_value * 83492791
    mixed = mixed ^ jnp.right_shift(mixed, 13)
    mixed = mixed * 1274126177
    mixed = mixed ^ jnp.right_shift(mixed, 16)
    uniform_value = (mixed & 65535).astype(jnp.float32) * (1.0 / 65536.0)
    return ((2.0 * uniform_value - 1.0) * math.sqrt(3.0 / total_coords)).astype(jnp.bfloat16)

def newton_inverse(fisher):
    width = fisher.shape[1]
    identity = jnp.eye(width, dtype=jnp.float32)
    trace_value = jnp.einsum('bii->b', fisher)
    damped = fisher + (DAMPING * trace_value)[:, None, None] * identity
    total = jnp.einsum('bii->b', damped)
    iterate = identity[None] / total[:, None, None]
    for _ in range(STEPS):
        product = jnp.einsum('bij,bjk->bik', damped, iterate, precision=lax.Precision.HIGHEST)
        iterate = jnp.einsum('bij,bjk->bik', iterate, 2.0 * identity - product, precision=lax.Precision.HIGHEST)
    return iterate

def reference(gradients, projection_seed, target_features):
    seed_value = projection_seed[0]

    def add_shard(shard, accumulated):
        first_col = (shard * COORD_DEV).astype(jnp.int32)
        grad_slab = lax.dynamic_slice_in_dim(gradients, first_col, COORD_DEV, 1)
        matrix = hashed(seed_value, first_col, COORD_DEV, 0, FEATS, COORDS)
        return accumulated + jnp.dot(grad_slab, matrix, preferred_element_type=jnp.float32)
    summed = lax.fori_loop(0, N_PARAM, add_shard, jnp.zeros((EXAMPLES, FEATS), jnp.float32))
    features = lax.optimization_barrier(summed.astype(jnp.bfloat16))
    widened = features.astype(jnp.float32).reshape(EXAMPLES, FEATS // BLOCK, BLOCK)
    fisher = jnp.einsum('ebi,ebj->bij', widened, widened, precision=lax.Precision.HIGHEST) / EXAMPLES
    inverse = newton_inverse(fisher)
    inverse_bf = lax.optimization_barrier(inverse.astype(jnp.bfloat16)).astype(jnp.float32)
    conditioned = jnp.einsum('ebm,bmj->ebj', widened, inverse_bf, precision=lax.Precision.HIGHEST)
    conditioned = conditioned.astype(jnp.bfloat16).reshape(EXAMPLES, FEATS)
    return jnp.dot(target_features, conditioned.T, preferred_element_type=jnp.float32)
```

```python
import functools
import math

import jax
import jax.numpy as jnp
from jax import lax
from jax.experimental import pallas as pl
from jax.experimental.pallas import tpu as pltpu
from jax.sharding import Mesh
from jax.sharding import PartitionSpec as P

FEATS = 4096
BLOCK = 128
STEPS = 10
DAMPING = 0.001

ROW_MUL = 73856093
COL_MUL = 19349663
SEED_MUL = 83492791
MIX_MUL = 1274126177
TOP_BIT = -(2**31)
HIGH_HALF = -65536

FEAT_TILE = 256
COORD_TILE = 2048
INIT_TILE = 256


def fold13(value):
    return value ^ jnp.right_shift(value, 13)


def project_kernel(seed_ref, grad_ref, own_ref, send_ref, rows_ref, *, scale):
    step = pl.program_id(0)
    coord_dev = grad_ref.shape[1]
    half = own_ref.shape[1]
    core = lax.axis_index("c")
    chip = lax.axis_index("z") * lax.axis_size("x") + lax.axis_index("x")
    row_start = (chip * lax.axis_size("c") + core) * coord_dev

    @pl.when(step == 0)
    def _():
        def fill(i, carry):
            start = pl.multiple_of(i * INIT_TILE, INIT_TILE)
            rows = lax.broadcasted_iota(jnp.int32, (INIT_TILE, 128), 0) + (row_start + start)
            rows_ref[pl.ds(start, INIT_TILE), :] = fold13(rows * ROW_MUL)
            return carry

        lax.fori_loop(0, coord_dev // INIT_TILE, fill, 0)

    columns = []
    for lane_tile in range(FEAT_TILE // 128):
        first = step * FEAT_TILE + lane_tile * 128
        col = first + lax.broadcasted_iota(jnp.int32, (1, 128), 1)
        columns.append(fold13(col * COL_MUL ^ seed_ref[0] * SEED_MUL) ^ TOP_BIT)

    def add_tile(i, total):
        start = pl.multiple_of(i * COORD_TILE, COORD_TILE)
        rows = rows_ref[pl.ds(start, COORD_TILE), :]
        tiles = []
        for column in columns:
            mixed = (rows ^ column) * MIX_MUL
            centred = (mixed ^ jnp.left_shift(mixed, 16)) & HIGH_HALF
            value = centred.astype(jnp.float32) * (scale * 2.0**-31)
            tiles.append(value.astype(jnp.bfloat16))
        return total + jnp.dot(
            grad_ref[:, pl.ds(start, COORD_TILE)],
            jnp.concatenate(tiles, 1),
            preferred_element_type=jnp.float32,
        )

    total = lax.fori_loop(
        0, coord_dev // COORD_TILE, add_tile, jnp.zeros((2 * half, FEAT_TILE), jnp.float32)
    )
    for j in range(FEAT_TILE // BLOCK):
        part = total[:, j * BLOCK : (j + 1) * BLOCK]

        @pl.when(core == 0)
        def _():
            own_ref[j] = part[:half]
            send_ref[j] = part[half:]

        @pl.when(core == 1)
        def _():
            own_ref[j] = part[half:]
            send_ref[j] = part[:half]


def project(gradients, projection_seed):
    exam_dev, coord_dev = gradients.shape
    total_coords = coord_dev * lax.axis_size(("z", "x", "c"))
    blocks = FEATS // BLOCK
    out = jax.ShapeDtypeStruct((blocks, exam_dev // 2, BLOCK), jnp.float32)
    block = pl.BlockSpec((FEAT_TILE // BLOCK, exam_dev // 2, BLOCK), lambda i, s: (i, 0, 0))
    return pl.pallas_call(
        functools.partial(project_kernel, scale=math.sqrt(3.0 / total_coords)),
        out_shape=[out, out],
        grid_spec=pltpu.PrefetchScalarGridSpec(
            num_scalar_prefetch=1,
            grid=(FEATS // FEAT_TILE,),
            in_specs=[pl.BlockSpec((exam_dev, coord_dev), lambda i, s: (0, 0))],
            out_specs=[block, block],
            scratch_shapes=[pltpu.VMEM((coord_dev, 128), jnp.int32)],
        ),
        compiler_params=pltpu.CompilerParams(
            dimension_semantics=("arbitrary",), vmem_limit_bytes=48 * 2**20
        ),
        name="project",
    )(projection_seed, gradients)


def dot_f32(a, b):
    return jnp.dot(a, b, precision=lax.Precision.HIGHEST, preferred_element_type=jnp.float32)


def score_kernel(feat_ref, target_ref, out_ref, picked_ref, sem):
    groups, half, width = feat_ref.shape
    chip = lax.axis_index("z") * lax.axis_size("x") + lax.axis_index("x")
    first = pl.multiple_of(chip * BLOCK, BLOCK)
    copy = pltpu.make_async_copy(
        target_ref.at[:, lax.axis_index("c"), :, pl.ds(first, BLOCK)], picked_ref, sem
    )
    copy.start()
    feats = feat_ref[...].reshape(groups * half, width)
    examples = groups * half
    fisher = lax.dot_general(
        feats, feats, (((0,), (0,)), ((), ())), preferred_element_type=jnp.float32
    ) / examples
    row = lax.broadcasted_iota(jnp.int32, (width, width), 0)
    col = lax.broadcasted_iota(jnp.int32, (width, width), 1)
    identity = (row == col).astype(jnp.float32)
    trace_value = jnp.sum(fisher * identity)
    damped = fisher + (DAMPING * trace_value) * identity
    total = jnp.sum(damped * identity)
    iterate = identity / total
    product = damped / total
    for step in range(STEPS):
        if step < STEPS - 1:
            both = jnp.concatenate([iterate, product], 0)
            both = 2.0 * both - dot_f32(both, product)
            iterate, product = both[:width], both[width:]
        else:
            iterate = 2.0 * iterate - dot_f32(iterate, product)
    inverse_bf = iterate.astype(jnp.bfloat16)
    mine = feat_ref[pl.ds(2 * lax.axis_index("y"), 2)].reshape(2 * half, width)
    conditioned = jnp.dot(mine, inverse_bf, preferred_element_type=jnp.float32).astype(jnp.bfloat16)
    copy.wait()
    picked = picked_ref[...].reshape(-1, width)
    partial = lax.dot_general(
        picked, conditioned, (((1,), (1,)), ((), ())), preferred_element_type=jnp.float32
    )
    out_ref[...] = partial.reshape(out_ref.shape).astype(out_ref.dtype)


def partial_scores(feats, targets):
    chips, cores, rows, _ = targets.shape
    return pl.pallas_call(
        score_kernel,
        out_shape=jax.ShapeDtypeStruct((chips, rows, 2 * feats.shape[1]), jnp.float32),
        in_specs=[pl.BlockSpec(memory_space=pltpu.VMEM), pl.BlockSpec(memory_space=pl.ANY)],
        out_specs=pl.BlockSpec(memory_space=pltpu.VMEM),
        scratch_shapes=[
            pltpu.VMEM((chips, rows, BLOCK), jnp.bfloat16),
            pltpu.SemaphoreType.DMA,
        ],
        name="scores",
    )(feats, targets)


def spread(array, axes):
    return lax.all_to_all(array, axes, split_axis=0, concat_axis=0, tiled=True)


def on_device(gradients, projection_seed, target_features):
    own, send = project(gradients, projection_seed)
    other = lax.ppermute(send, "c", [(0, 1), (1, 0)])
    chip_sum = (own + other).astype(jnp.bfloat16)
    pieces = spread(chip_sum, ("z", "x"))
    feats = jnp.sum(pieces.astype(jnp.float32), 0).astype(jnp.bfloat16)
    groups = lax.axis_size(("y", "c"))
    every = spread(jnp.broadcast_to(feats[None], (groups, *feats.shape)), ("y", "c"))
    chips = lax.axis_size(("z", "x"))
    rows = target_features.shape[0] // (2 * chips)
    partial = partial_scores(every, target_features.reshape(chips, 2, rows, FEATS))
    return jnp.sum(spread(partial, ("z", "x")), 0)


def solution(mesh):
    size = mesh.shape["param"]
    z, x, c, y = 8, 4, 2, mesh.shape["ex"]
    assert z * x * c == size
    inner = Mesh(mesh.devices.reshape(z, x, c, y), ("z", "x", "c", "y"))
    param = ("z", "x", "c")
    return jax.shard_map(
        on_device,
        mesh=inner,
        in_specs=(P("y", param), P(), P()),
        out_specs=P(param, "y"),
        check_vma=False,
    )
```

```python
import functools
import math

import jax
import jax.numpy as jnp
from jax import lax
from jax.experimental import pallas as pl
from jax.experimental.pallas import tpu as pltpu
from jax.sharding import Mesh
from jax.sharding import PartitionSpec as P

PARAM = ("z", "xh", "xl", "c")
CHIPS = ("z", "xh", "xl")

FEATS = 4096
BLOCK = 128
STEPS = 10
DAMPING = 0.001

ROW_MUL = 73856093
COL_MUL = 19349663
SEED_MUL = 83492791
MIX_MUL = 1274126177
TOP_BIT = -(2**31)
HIGH_HALF = -65536

FEAT_TILE = 256
COORD_TILE = 2048
INIT_TILE = 256


def fold13(value):
    return value ^ jnp.right_shift(value, 13)


def project_kernel(seed_ref, grad_ref, own_ref, send_ref, rows_ref, *, scale, first_feat):
    step = pl.program_id(0)
    coord_dev = grad_ref.shape[1]
    half = own_ref.shape[1]
    core = lax.axis_index("c")
    row_start = lax.axis_index(PARAM) * coord_dev

    @pl.when(step == 0)
    def _():
        def fill(i, carry):
            start = pl.multiple_of(i * INIT_TILE, INIT_TILE)
            rows = lax.broadcasted_iota(jnp.int32, (INIT_TILE, 128), 0) + (row_start + start)
            rows_ref[pl.ds(start, INIT_TILE), :] = fold13(rows * ROW_MUL)
            return carry

        lax.fori_loop(0, coord_dev // INIT_TILE, fill, 0)

    columns = []
    for lane_tile in range(FEAT_TILE // 128):
        first = first_feat + step * FEAT_TILE + lane_tile * 128
        col = first + lax.broadcasted_iota(jnp.int32, (1, 128), 1)
        columns.append(fold13(col * COL_MUL ^ seed_ref[0] * SEED_MUL) ^ TOP_BIT)

    def add_tile(i, total):
        start = pl.multiple_of(i * COORD_TILE, COORD_TILE)
        rows = rows_ref[pl.ds(start, COORD_TILE), :]
        tiles = []
        for column in columns:
            mixed = (rows ^ column) * MIX_MUL
            centred = (mixed ^ jnp.left_shift(mixed, 16)) & HIGH_HALF
            value = centred.astype(jnp.float32) * (scale * 2.0**-31)
            tiles.append(value.astype(jnp.bfloat16))
        return total + jnp.dot(
            grad_ref[:, pl.ds(start, COORD_TILE)],
            jnp.concatenate(tiles, 1),
            preferred_element_type=jnp.float32,
        )

    total = lax.fori_loop(
        0, coord_dev // COORD_TILE, add_tile, jnp.zeros((2 * half, FEAT_TILE), jnp.float32)
    )
    for j in range(FEAT_TILE // BLOCK):
        part = total[:, j * BLOCK : (j + 1) * BLOCK]

        @pl.when(core == 0)
        def _():
            own_ref[j] = part[:half]
            send_ref[j] = part[half:]

        @pl.when(core == 1)
        def _():
            own_ref[j] = part[half:]
            send_ref[j] = part[:half]


def project(gradients, projection_seed, first_feat, feats):
    exam_dev, coord_dev = gradients.shape
    total_coords = coord_dev * lax.axis_size(PARAM)
    blocks = feats // BLOCK
    out = jax.ShapeDtypeStruct((blocks, exam_dev // 2, BLOCK), jnp.float32)
    block = pl.BlockSpec((FEAT_TILE // BLOCK, exam_dev // 2, BLOCK), lambda i, s: (i, 0, 0))
    return pl.pallas_call(
        functools.partial(
            project_kernel, scale=math.sqrt(3.0 / total_coords), first_feat=first_feat
        ),
        out_shape=[out, out],
        grid_spec=pltpu.PrefetchScalarGridSpec(
            num_scalar_prefetch=1,
            grid=(feats // FEAT_TILE,),
            in_specs=[pl.BlockSpec((exam_dev, coord_dev), lambda i, s: (0, 0))],
            out_specs=[block, block],
            scratch_shapes=[pltpu.VMEM((coord_dev, 128), jnp.int32)],
        ),
        compiler_params=pltpu.CompilerParams(
            dimension_semantics=("arbitrary",), vmem_limit_bytes=48 * 2**20
        ),
        cost_estimate=pl.CostEstimate(
            flops=2 * exam_dev * coord_dev * feats,
            bytes_accessed=2 * coord_dev * feats,
            transcendentals=0,
        ),
        name="project",
    )(projection_seed, gradients)


def dot_f32(a, b):
    return jnp.dot(a, b, precision=lax.Precision.HIGHEST, preferred_element_type=jnp.float32)


def score_kernel(feat_ref, target_ref, out_ref, picked_ref, sem):
    groups, part, width = feat_ref.shape
    block = lax.axis_index(("xl", "z", "xh"))
    first = pl.multiple_of(block * BLOCK, BLOCK)
    copy = pltpu.make_async_copy(
        target_ref.at[:, lax.axis_index("c"), :, pl.ds(first, BLOCK)], picked_ref, sem
    )
    copy.start()
    feats = feat_ref[...].reshape(groups * part, width)
    examples = groups * part
    fisher = lax.dot_general(
        feats, feats, (((0,), (0,)), ((), ())), preferred_element_type=jnp.float32
    ) / examples
    row = lax.broadcasted_iota(jnp.int32, (width, width), 0)
    col = lax.broadcasted_iota(jnp.int32, (width, width), 1)
    identity = (row == col).astype(jnp.float32)
    trace_value = jnp.sum(fisher * identity)
    damped = fisher + (DAMPING * trace_value) * identity
    total = jnp.sum(damped * identity)
    iterate = identity / total
    product = damped / total
    for step in range(STEPS):
        if step < STEPS - 1:
            both = jnp.concatenate([iterate, product], 0)
            both = 2.0 * both - dot_f32(both, product)
            iterate, product = both[:width], both[width:]
        else:
            iterate = 2.0 * iterate - dot_f32(iterate, product)
    inverse_bf = iterate.astype(jnp.bfloat16)
    base = 4 * lax.axis_index("y")
    mine = jnp.concatenate([feat_ref[base + i] for i in (0, 2, 1, 3)], 0)
    conditioned = jnp.dot(mine, inverse_bf, preferred_element_type=jnp.float32).astype(jnp.bfloat16)
    copy.wait()
    picked = picked_ref[...].reshape(-1, width)
    partial = lax.dot_general(
        picked, conditioned, (((1,), (1,)), ((), ())), preferred_element_type=jnp.float32
    )
    out_ref[...] = partial.reshape(out_ref.shape).astype(out_ref.dtype)


def partial_scores(feats, targets):
    chips, _, rows, _ = targets.shape
    return pl.pallas_call(
        score_kernel,
        out_shape=jax.ShapeDtypeStruct((chips, rows, 4 * feats.shape[1]), jnp.bfloat16),
        in_specs=[pl.BlockSpec(memory_space=pltpu.VMEM), pl.BlockSpec(memory_space=pl.ANY)],
        out_specs=pl.BlockSpec(memory_space=pltpu.VMEM),
        scratch_shapes=[
            pltpu.VMEM((chips, rows, BLOCK), jnp.bfloat16),
            pltpu.SemaphoreType.DMA,
        ],
        name="scores",
    )(feats, targets)


def spread(array, axes):
    return lax.all_to_all(array, axes, split_axis=0, concat_axis=0, tiled=True)


def reduced(gradients, projection_seed, part):
    feats = FEATS // 2
    own, send = project(gradients, projection_seed, part * feats, feats)
    other = lax.ppermute(send, "c", [(0, 1), (1, 0)])
    chip_sum = (own + other).astype(jnp.bfloat16)
    chips = lax.axis_size(CHIPS)
    pieces = spread(chip_sum.reshape(chips, -1, BLOCK), CHIPS)
    return jnp.sum(pieces.astype(jnp.float32), 0).astype(jnp.bfloat16)


def on_device(gradients, projection_seed, target_features):
    both = jnp.stack([reduced(gradients, projection_seed, part) for part in range(2)])
    _, part, width = both.shape
    sent = jnp.broadcast_to(both[None, :, None], (lax.axis_size("y"), 2, 2, part, width))
    every = spread(sent.reshape(-1, part, width), ("y", "xl", "c"))
    chips = lax.axis_size(CHIPS)
    rows = target_features.shape[0] // (2 * chips)
    partial = partial_scores(every, target_features.reshape(chips, 2, rows, FEATS))
    return jnp.sum(spread(partial, CHIPS).astype(jnp.float32), 0)


def solution(mesh):
    z, xh, xl, c, y = 8, 2, 2, 2, mesh.shape["ex"]
    assert z * xh * xl * c == mesh.shape["param"]
    inner = Mesh(mesh.devices.reshape(z, xh, xl, c, y), (*PARAM, "y"))
    return jax.shard_map(
        on_device,
        mesh=inner,
        in_specs=(P("y", PARAM), P(), P()),
        out_specs=P(PARAM, "y"),
        check_vma=False,
    )
```

```python
import functools
import math

import jax
import jax.numpy as jnp
from jax import lax
from jax.experimental import pallas as pl
from jax.experimental.pallas import tpu as pltpu
from jax.sharding import Mesh
from jax.sharding import PartitionSpec as P

PARAM = ("z", "x", "c")
CHIPS = ("z", "x")

FEATS = 4096
BLOCK = 128
STEPS = 10
DAMPING = 0.001

ROW_MUL = 73856093
COL_MUL = 19349663
SEED_MUL = 83492791
MIX_MUL = 1274126177
TOP_BIT = -(2**31)
HIGH_HALF = -65536

FEAT_TILE = 512
INIT_TILE = 256


def fold13(value):
    return value ^ jnp.right_shift(value, 13)


def project_kernel(
    seed_ref, grad_ref, target_ref, own_ref, send_ref, picked_ref, rows_ref, held_ref, sems, *, scale
):
    step = pl.program_id(0)
    coord_dev = grad_ref.shape[1]
    half = own_ref.shape[1]
    core = lax.axis_index("c")
    row_start = lax.axis_index(PARAM) * coord_dev

    def pick():
        first = pl.multiple_of(lax.axis_index(CHIPS) * BLOCK, BLOCK)
        part = target_ref.at[:, core, :, pl.ds(first, BLOCK)]
        return pltpu.make_async_copy(part, picked_ref, sems.at[1])

    @pl.when(step == 0)
    def _():
        copy = pltpu.make_async_copy(grad_ref, held_ref, sems.at[0])
        copy.start()
        pick().start()

        def fill(i, carry):
            start = pl.multiple_of(i * INIT_TILE, INIT_TILE)
            rows = lax.broadcasted_iota(jnp.int32, (INIT_TILE, 128), 0) + (row_start + start)
            rows_ref[pl.ds(start, INIT_TILE), :] = fold13(rows * ROW_MUL)
            return carry

        lax.fori_loop(0, coord_dev // INIT_TILE, fill, 0)
        copy.wait()

    columns = []
    for lane_tile in range(FEAT_TILE // 128):
        first = step * FEAT_TILE + lane_tile * 128
        col = first + lax.broadcasted_iota(jnp.int32, (1, 128), 1)
        columns.append(fold13(col * COL_MUL ^ seed_ref[0] * SEED_MUL) ^ TOP_BIT)

    rows = rows_ref[...]
    tiles = []
    for column in columns:
        mixed = (rows ^ column) * MIX_MUL
        centred = (mixed ^ jnp.left_shift(mixed, 16)) & HIGH_HALF
        value = centred.astype(jnp.float32) * (scale * 2.0**-31)
        tiles.append(value.astype(jnp.bfloat16))
    total = jnp.dot(
        held_ref[...], jnp.concatenate(tiles, 1), preferred_element_type=jnp.float32
    )
    for j in range(FEAT_TILE // BLOCK):
        part = total[:, j * BLOCK : (j + 1) * BLOCK]

        @pl.when(core == 0)
        def _():
            own_ref[j] = part[:half]
            send_ref[j] = part[half:]

        @pl.when(core == 1)
        def _():
            own_ref[j] = part[half:]
            send_ref[j] = part[:half]

    @pl.when(step == pl.num_programs(0) - 1)
    def _():
        pick().wait()


def project(gradients, projection_seed, targets):
    chips, _, rows, _ = targets.shape
    exam_dev, coord_dev = gradients.shape
    total_coords = coord_dev * lax.axis_size(PARAM)
    blocks = FEATS // BLOCK
    out = jax.ShapeDtypeStruct((blocks, exam_dev // 2, BLOCK), jnp.float32)
    block = pl.BlockSpec((FEAT_TILE // BLOCK, exam_dev // 2, BLOCK), lambda i, s: (i, 0, 0))
    return pl.pallas_call(
        functools.partial(project_kernel, scale=math.sqrt(3.0 / total_coords)),
        out_shape=[out, out, jax.ShapeDtypeStruct((chips, rows, BLOCK), targets.dtype)],
        grid_spec=pltpu.PrefetchScalarGridSpec(
            num_scalar_prefetch=1,
            grid=(FEATS // FEAT_TILE,),
            in_specs=[pl.BlockSpec(memory_space=pl.ANY)] * 2,
            out_specs=[block, block, pl.BlockSpec((chips, rows, BLOCK), lambda i, s: (0, 0, 0))],
            scratch_shapes=[
                pltpu.VMEM((coord_dev, 128), jnp.int32),
                pltpu.VMEM((exam_dev, coord_dev), gradients.dtype),
                pltpu.SemaphoreType.DMA((2,)),
            ],
        ),
        compiler_params=pltpu.CompilerParams(
            dimension_semantics=("arbitrary",), vmem_limit_bytes=60 * 2**20
        ),
        name="project",
    )(projection_seed, gradients, targets)


def dot_f32(a, b):
    return jnp.dot(a, b, precision=lax.Precision.HIGHEST, preferred_element_type=jnp.float32)


def score_kernel(mine_ref, next_ref, across_ref, last_ref, picked_ref, out_ref):
    _, half, width = mine_ref.shape
    core = lax.axis_index("c")
    mine = jnp.concatenate([mine_ref[core], mine_ref[1 - core]], 0)
    others = [ref[...].reshape(2 * half, width) for ref in (next_ref, across_ref, last_ref)]
    feats = jnp.concatenate([mine, *others], 0)
    examples = feats.shape[0]
    fisher = lax.dot_general(
        feats, feats, (((0,), (0,)), ((), ())), preferred_element_type=jnp.float32
    ) / examples
    row = lax.broadcasted_iota(jnp.int32, (width, width), 0)
    col = lax.broadcasted_iota(jnp.int32, (width, width), 1)
    identity = (row == col).astype(jnp.float32)
    trace_value = jnp.sum(fisher * identity)
    damped = fisher + (DAMPING * trace_value) * identity
    total = jnp.sum(damped * identity)
    iterate = identity / total
    product = damped / total
    for step in range(STEPS):
        if step < STEPS - 1:
            both = jnp.concatenate([iterate, product], 0)
            both = 2.0 * both - dot_f32(both, product)
            iterate, product = both[:width], both[width:]
        else:
            iterate = 2.0 * iterate - dot_f32(iterate, product)
    inverse_bf = iterate.astype(jnp.bfloat16)
    conditioned = jnp.dot(mine, inverse_bf, preferred_element_type=jnp.float32).astype(jnp.bfloat16)
    picked = picked_ref[...].reshape(-1, width)
    partial = lax.dot_general(
        picked, conditioned, (((1,), (1,)), ((), ())), preferred_element_type=jnp.float32
    )
    out_ref[...] = partial.reshape(out_ref.shape).astype(out_ref.dtype)


def partial_scores(mine, others, picked):
    chips, rows, _ = picked.shape
    vmem = pl.BlockSpec(memory_space=pltpu.VMEM)
    return pl.pallas_call(
        score_kernel,
        out_shape=jax.ShapeDtypeStruct((chips, rows, 2 * mine.shape[1]), jnp.bfloat16),
        in_specs=[vmem] * 5,
        out_specs=vmem,
        compiler_params=pltpu.CompilerParams(vmem_limit_bytes=8 * 2**20),
        name="scores",
    )(mine, *others, picked)


def exchange(array, axis, distance):
    return lax.ppermute(array, axis, [(i, i ^ distance) for i in range(lax.axis_size(axis))])


def spread(array, axes):
    return lax.all_to_all(array, axes, split_axis=0, concat_axis=0, tiled=True)


def on_device(gradients, projection_seed, target_features):
    chips = lax.axis_size(CHIPS)
    rows = target_features.shape[0] // (2 * chips)
    targets = target_features.reshape(chips, 2, rows, FEATS)
    own, send, picked = project(gradients, projection_seed, targets)
    chip_sum = (own + exchange(send, "c", 1)).astype(jnp.bfloat16)
    pieces = spread(chip_sum, CHIPS)
    feats = jnp.sum(pieces.astype(jnp.float32), 0).astype(jnp.bfloat16)
    mine = jnp.stack([feats, exchange(feats, "c", 1)])
    others = [exchange(mine, "y", distance) for distance in (1, 3, 2)]
    partial = partial_scores(mine, others, picked)
    return jnp.sum(spread(partial, CHIPS).astype(jnp.float32), 0)


def solution(mesh):
    z, x, c, y = 8, 4, 2, mesh.shape["ex"]
    assert z * x * c == mesh.shape["param"]
    inner = Mesh(mesh.devices.reshape(z, x, c, y), (*PARAM, "y"))
    return jax.shard_map(
        on_device,
        mesh=inner,
        in_specs=(P("y", PARAM), P(), P()),
        out_specs=P(PARAM, "y"),
        check_vma=False,
    )
```

```python
import functools
import math

import jax
import jax.numpy as jnp
from jax import lax
from jax.experimental import pallas as pl
from jax.experimental.pallas import tpu as pltpu
from jax.sharding import Mesh
from jax.sharding import PartitionSpec as P

PARAM = ("z", "x", "c")
CHIPS = ("z", "x")

FEATS = 4096
BLOCK = 128
STEPS = 10
DAMPING = 0.001

ROW_MUL = 73856093
COL_MUL = 19349663
SEED_MUL = 83492791
MIX_MUL = 1274126177
TOP_BIT = -(2**31)
HIGH_HALF = -65536

FEAT_TILE = 512
INIT_TILE = 256


def fold13(value):
    return value ^ jnp.right_shift(value, 13)


def project_kernel(
    seed_ref, grad_ref, target_ref, own_ref, send_ref, picked_ref, rows_ref, held_ref, sems, *, scale
):
    step = pl.program_id(0)
    coord_dev = grad_ref.shape[1]
    half = own_ref.shape[1]
    core = lax.axis_index("c")
    row_start = lax.axis_index(PARAM) * coord_dev

    def pick():
        first = pl.multiple_of(lax.axis_index(CHIPS) * BLOCK, BLOCK)
        part = target_ref.at[:, core, :, pl.ds(first, BLOCK)]
        return pltpu.make_async_copy(part, picked_ref, sems.at[1])

    @pl.when(step == 0)
    def _():
        copy = pltpu.make_async_copy(grad_ref, held_ref, sems.at[0])
        copy.start()
        pick().start()

        def fill(i, carry):
            start = pl.multiple_of(i * INIT_TILE, INIT_TILE)
            rows = lax.broadcasted_iota(jnp.int32, (INIT_TILE, 128), 0) + (row_start + start)
            rows_ref[pl.ds(start, INIT_TILE), :] = fold13(rows * ROW_MUL)
            return carry

        lax.fori_loop(0, coord_dev // INIT_TILE, fill, 0)
        copy.wait()

    columns = []
    for lane_tile in range(FEAT_TILE // 128):
        first = step * FEAT_TILE + lane_tile * 128
        col = first + lax.broadcasted_iota(jnp.int32, (1, 128), 1)
        columns.append(fold13(col * COL_MUL ^ seed_ref[0] * SEED_MUL) ^ TOP_BIT)

    rows = rows_ref[...]
    tiles = []
    for column in columns:
        mixed = (rows ^ column) * MIX_MUL
        centred = (mixed ^ jnp.left_shift(mixed, 16)) & HIGH_HALF
        tiles.append(centred.astype(jnp.float32).astype(jnp.bfloat16))
    total = jnp.dot(
        held_ref[...], jnp.concatenate(tiles, 1), preferred_element_type=jnp.float32
    ) * (scale * 2.0**-31)
    block = step * (FEAT_TILE // BLOCK)
    for j in range(FEAT_TILE // BLOCK):
        part = total[:, j * BLOCK : (j + 1) * BLOCK]

        @pl.when(core == 0)
        def _():
            own_ref[block + j] = part[:half]
            send_ref[block + j] = part[half:]

        @pl.when(core == 1)
        def _():
            own_ref[block + j] = part[half:]
            send_ref[block + j] = part[:half]

    @pl.when(step == pl.num_programs(0) - 1)
    def _():
        pick().wait()


def project(gradients, projection_seed, targets):
    chips, _, rows, _ = targets.shape
    exam_dev, coord_dev = gradients.shape
    total_coords = coord_dev * lax.axis_size(PARAM)
    blocks = FEATS // BLOCK
    out = jax.ShapeDtypeStruct((blocks, exam_dev // 2, BLOCK), jnp.float32)
    vmem = pl.BlockSpec(memory_space=pltpu.VMEM)
    return pl.pallas_call(
        functools.partial(project_kernel, scale=math.sqrt(3.0 / total_coords)),
        out_shape=[out, out, jax.ShapeDtypeStruct((chips, rows, BLOCK), targets.dtype)],
        grid_spec=pltpu.PrefetchScalarGridSpec(
            num_scalar_prefetch=1,
            grid=(FEATS // FEAT_TILE,),
            in_specs=[pl.BlockSpec(memory_space=pl.ANY)] * 2,
            out_specs=[vmem] * 3,
            scratch_shapes=[
                pltpu.VMEM((coord_dev, 128), jnp.int32),
                pltpu.VMEM((exam_dev, coord_dev), gradients.dtype),
                pltpu.SemaphoreType.DMA((2,)),
            ],
        ),
        compiler_params=pltpu.CompilerParams(
            dimension_semantics=("arbitrary",), vmem_limit_bytes=50 * 2**20
        ),
        name="project",
    )(projection_seed, gradients, targets)


def dot_f32(a, b):
    return jnp.dot(a, b, precision=lax.Precision.HIGHEST, preferred_element_type=jnp.float32)


def score_kernel(mine_ref, beside_ref, across_ref, far_ref, picked_ref, out_ref):
    _, half, width = mine_ref.shape
    core = lax.axis_index("c")
    mine = jnp.concatenate([mine_ref[core], mine_ref[1 - core]], 0)
    others = [ref[...].reshape(2 * half, width) for ref in (beside_ref, across_ref, far_ref)]
    feats = jnp.concatenate([mine, *others], 0)
    examples = feats.shape[0]
    fisher = lax.dot_general(
        feats, feats, (((0,), (0,)), ((), ())), preferred_element_type=jnp.float32
    ) / examples
    row = lax.broadcasted_iota(jnp.int32, (width, width), 0)
    col = lax.broadcasted_iota(jnp.int32, (width, width), 1)
    identity = (row == col).astype(jnp.float32)
    trace_value = jnp.sum(fisher * identity)
    damped = fisher + (DAMPING * trace_value) * identity
    total = jnp.sum(damped * identity)
    iterate = identity / total
    product = damped / total
    for step in range(STEPS):
        if step < STEPS - 1:
            both = jnp.concatenate([iterate, product], 0)
            both = 2.0 * both - dot_f32(both, product)
            iterate, product = both[:width], both[width:]
        else:
            iterate = 2.0 * iterate - dot_f32(iterate, product)
    inverse_bf = iterate.astype(jnp.bfloat16)
    conditioned = jnp.dot(mine, inverse_bf, preferred_element_type=jnp.float32).astype(jnp.bfloat16)
    picked = picked_ref[...].reshape(-1, width)
    partial = lax.dot_general(
        picked, conditioned, (((1,), (1,)), ((), ())), preferred_element_type=jnp.float32
    )
    out_ref[...] = partial.reshape(out_ref.shape).astype(out_ref.dtype)


def partial_scores(mine, others, picked):
    chips, rows, _ = picked.shape
    vmem = pl.BlockSpec(memory_space=pltpu.VMEM)
    return pl.pallas_call(
        score_kernel,
        out_shape=jax.ShapeDtypeStruct((chips, rows, 2 * mine.shape[1]), jnp.bfloat16),
        in_specs=[vmem] * 5,
        out_specs=vmem,
        compiler_params=pltpu.CompilerParams(vmem_limit_bytes=8 * 2**20),
        name="scores",
    )(mine, *others, picked)


def exchange(array, axis, distance):
    return lax.ppermute(array, axis, [(i, i ^ distance) for i in range(lax.axis_size(axis))])


def spread(array, axes):
    return lax.all_to_all(array, axes, split_axis=0, concat_axis=0, tiled=True)


def on_device(gradients, projection_seed, target_features):
    chips = lax.axis_size(CHIPS)
    rows = target_features.shape[0] // (2 * chips)
    targets = target_features.reshape(chips, 2, rows, FEATS)
    own, send, picked = project(gradients, projection_seed, targets)
    chip_sum = (own + exchange(send, "c", 1)).astype(jnp.bfloat16)
    pieces = spread(chip_sum, CHIPS)
    feats = jnp.sum(pieces.astype(jnp.float32), 0).astype(jnp.bfloat16)
    mine = jnp.stack([feats, exchange(feats, "c", 1)])
    beside = exchange(mine, "y", 1)
    others = [beside, exchange(mine, "y", 3), exchange(beside, "y", 3)]
    partial = partial_scores(mine, others, picked)
    return jnp.sum(spread(partial, CHIPS).astype(jnp.float32), 0)


def solution(mesh):
    z, x, c, y = 8, 4, 2, mesh.shape["ex"]
    assert z * x * c == mesh.shape["param"]
    inner = Mesh(mesh.devices.reshape(z, x, c, y), (*PARAM, "y"))
    return jax.shard_map(
        on_device,
        mesh=inner,
        in_specs=(P("y", PARAM), P(), P()),
        out_specs=P(PARAM, "y"),
        check_vma=False,
    )
```

```python
import functools
import math

import jax
import jax.numpy as jnp
from jax import lax
from jax.experimental import pallas as pl
from jax.experimental.pallas import tpu as pltpu
from jax.sharding import Mesh
from jax.sharding import PartitionSpec as P

PARAM = ("z", "x", "c")
CHIPS = ("z", "x")

FEATS = 4096
BLOCK = 128
STEPS = 10
DAMPING = 0.001

ROW_MUL = 73856093
COL_MUL = 19349663
SEED_MUL = 83492791
MIX_MUL = 1274126177
TOP_BIT = -(2**31)
HIGH_HALF = -65536

FEAT_TILE = 1024
INIT_TILE = 256


def fold13(value):
    return value ^ jnp.right_shift(value, 13)


def project_kernel(
    seed_ref, grad_ref, target_ref, own_ref, send_ref, picked_ref, rows_ref, held_ref, sems, *, scale
):
    step = pl.program_id(0)
    coord_dev = grad_ref.shape[1]
    half = own_ref.shape[1]
    core = lax.axis_index("c")
    row_start = lax.axis_index(PARAM) * coord_dev

    def pick():
        first = pl.multiple_of(lax.axis_index(CHIPS) * BLOCK, BLOCK)
        part = target_ref.at[:, core, :, pl.ds(first, BLOCK)]
        return pltpu.make_async_copy(part, picked_ref, sems.at[1])

    @pl.when(step == 0)
    def _():
        copy = pltpu.make_async_copy(grad_ref, held_ref, sems.at[0])
        copy.start()
        pick().start()

        def fill(i, carry):
            start = pl.multiple_of(i * INIT_TILE, INIT_TILE)
            rows = lax.broadcasted_iota(jnp.int32, (INIT_TILE, 128), 0) + (row_start + start)
            rows_ref[pl.ds(start, INIT_TILE), :] = fold13(rows * ROW_MUL)
            return carry

        lax.fori_loop(0, coord_dev // INIT_TILE, fill, 0)
        copy.wait()

    columns = []
    for lane_tile in range(FEAT_TILE // 128):
        first = step * FEAT_TILE + lane_tile * 128
        col = first + lax.broadcasted_iota(jnp.int32, (1, 128), 1)
        columns.append(fold13(col * COL_MUL ^ seed_ref[0] * SEED_MUL) ^ TOP_BIT)

    rows = rows_ref[...]
    tiles = []
    for column in columns:
        mixed = (rows ^ column) * MIX_MUL
        centred = (mixed ^ jnp.left_shift(mixed, 16)) & HIGH_HALF
        tiles.append(centred.astype(jnp.float32).astype(jnp.bfloat16))
    total = jnp.dot(
        held_ref[...], jnp.concatenate(tiles, 1), preferred_element_type=jnp.float32
    ) * (scale * 2.0**-31)
    block = step * (FEAT_TILE // BLOCK)
    for j in range(FEAT_TILE // BLOCK):
        part = total[:, j * BLOCK : (j + 1) * BLOCK]

        @pl.when(core == 0)
        def _():
            own_ref[block + j] = part[:half]
            send_ref[block + j] = part[half:].astype(send_ref.dtype)

        @pl.when(core == 1)
        def _():
            own_ref[block + j] = part[half:]
            send_ref[block + j] = part[:half].astype(send_ref.dtype)

    @pl.when(step == pl.num_programs(0) - 1)
    def _():
        pick().wait()


def project(gradients, projection_seed, targets):
    chips, _, rows, _ = targets.shape
    exam_dev, coord_dev = gradients.shape
    total_coords = coord_dev * lax.axis_size(PARAM)
    blocks = FEATS // BLOCK
    own = jax.ShapeDtypeStruct((blocks, exam_dev // 2, BLOCK), jnp.float32)
    send = jax.ShapeDtypeStruct(own.shape, jnp.bfloat16)
    vmem = pl.BlockSpec(memory_space=pltpu.VMEM)
    return pl.pallas_call(
        functools.partial(project_kernel, scale=math.sqrt(3.0 / total_coords)),
        out_shape=[own, send, jax.ShapeDtypeStruct((chips, rows, BLOCK), targets.dtype)],
        grid_spec=pltpu.PrefetchScalarGridSpec(
            num_scalar_prefetch=1,
            grid=(FEATS // FEAT_TILE,),
            in_specs=[pl.BlockSpec(memory_space=pl.ANY)] * 2,
            out_specs=[vmem] * 3,
            scratch_shapes=[
                pltpu.VMEM((coord_dev, 128), jnp.int32),
                pltpu.VMEM((exam_dev, coord_dev), gradients.dtype),
                pltpu.SemaphoreType.DMA((2,)),
            ],
        ),
        compiler_params=pltpu.CompilerParams(
            dimension_semantics=("arbitrary",), vmem_limit_bytes=52 * 2**20
        ),
        name="project",
    )(projection_seed, gradients, targets)


def split_bf16(value):
    high = value.astype(jnp.bfloat16)
    return high, (value - high.astype(jnp.float32)).astype(jnp.bfloat16)


def dot_split(a, b):
    a_high, a_low = split_bf16(a)
    b_high, b_low = split_bf16(b)
    rows = a.shape[0]
    tall = jnp.dot(
        jnp.concatenate([a_high, a_low], 0), b_high, preferred_element_type=jnp.float32
    )
    return tall[:rows] + (
        tall[rows:] + jnp.dot(a_high, b_low, preferred_element_type=jnp.float32)
    )


def score_kernel(mine_ref, beside_ref, across_ref, far_ref, picked_ref, out_ref):
    _, half, width = mine_ref.shape
    core = lax.axis_index("c")
    mine = jnp.concatenate([mine_ref[core], mine_ref[1 - core]], 0)
    others = [ref[...].reshape(2 * half, width) for ref in (beside_ref, across_ref, far_ref)]
    feats = jnp.concatenate([mine, *others], 0)
    examples = feats.shape[0]
    fisher = lax.dot_general(
        feats, feats, (((0,), (0,)), ((), ())), preferred_element_type=jnp.float32
    ) / examples
    row = lax.broadcasted_iota(jnp.int32, (width, width), 0)
    col = lax.broadcasted_iota(jnp.int32, (width, width), 1)
    identity = (row == col).astype(jnp.float32)
    trace_value = jnp.sum(fisher * identity)
    damped = fisher + (DAMPING * trace_value) * identity
    total = jnp.sum(damped * identity)
    iterate = identity / total
    product = damped / total
    for step in range(STEPS):
        if step < STEPS - 1:
            both = jnp.concatenate([iterate, product], 0)
            both = 2.0 * both - dot_split(both, product)
            iterate, product = both[:width], both[width:]
        else:
            iterate = 2.0 * iterate - dot_split(iterate, product)
    inverse_bf = iterate.astype(jnp.bfloat16)
    conditioned = jnp.dot(mine, inverse_bf, preferred_element_type=jnp.float32).astype(jnp.bfloat16)
    picked = picked_ref[...].reshape(-1, width)
    partial = lax.dot_general(
        picked, conditioned, (((1,), (1,)), ((), ())), preferred_element_type=jnp.float32
    )
    out_ref[...] = partial.reshape(out_ref.shape).astype(out_ref.dtype)


def partial_scores(mine, others, picked):
    chips, rows, _ = picked.shape
    vmem = pl.BlockSpec(memory_space=pltpu.VMEM)
    return pl.pallas_call(
        score_kernel,
        out_shape=jax.ShapeDtypeStruct((chips, rows, 2 * mine.shape[1]), jnp.bfloat16),
        in_specs=[vmem] * 5,
        out_specs=vmem,
        compiler_params=pltpu.CompilerParams(vmem_limit_bytes=8 * 2**20),
        name="scores",
    )(mine, *others, picked)


def exchange(array, axis, distance):
    return lax.ppermute(array, axis, [(i, i ^ distance) for i in range(lax.axis_size(axis))])


def spread(array, axes):
    return lax.all_to_all(array, axes, split_axis=0, concat_axis=0, tiled=True)


def on_device(gradients, projection_seed, target_features):
    chips = lax.axis_size(CHIPS)
    rows = target_features.shape[0] // (2 * chips)
    targets = target_features.reshape(chips, 2, rows, FEATS)
    own, send, picked = project(gradients, projection_seed, targets)
    chip_sum = (own + exchange(send, "c", 1)).astype(jnp.bfloat16)
    pieces = spread(chip_sum, CHIPS)
    feats = jnp.sum(pieces.astype(jnp.float32), 0).astype(jnp.bfloat16)
    mine = jnp.stack([feats, exchange(feats, "c", 1)])
    others = [exchange(mine, "y", distance) for distance in (1, 3, 2)]
    partial = partial_scores(mine, others, picked)
    return jnp.sum(spread(partial, CHIPS).astype(jnp.float32), 0)


def solution(mesh):
    z, x, c, y = 8, 4, 2, mesh.shape["ex"]
    assert z * x * c == mesh.shape["param"]
    inner = Mesh(mesh.devices.reshape(z, x, c, y), (*PARAM, "y"))
    return jax.shard_map(
        on_device,
        mesh=inner,
        in_specs=(P("y", PARAM), P(), P()),
        out_specs=P(PARAM, "y"),
        check_vma=False,
    )
```

```python
import functools
import math

import jax
import jax.numpy as jnp
from jax import lax
from jax.experimental import pallas as pl
from jax.experimental.pallas import tpu as pltpu
from jax.sharding import Mesh
from jax.sharding import PartitionSpec as P

PARAM = ("z", "x", "c")
CHIPS = ("z", "x")

FEATS = 4096
BLOCK = 128
STEPS = 10
DAMPING = 0.001

ROW_MUL = 73856093
COL_MUL = 19349663
SEED_MUL = 83492791
MIX_MUL = 1274126177
TOP_BIT = -(2**31)
HIGH_HALF = -65536

FEAT_TILE = 512


def fold13(value):
    return value ^ jnp.right_shift(value, 13)


def project_kernel(
    seed_ref,
    grad_ref,
    target_ref,
    own_ref,
    send_ref,
    picked_ref,
    mixed_rows_ref,
    landed_ref,
    held_ref,
    sems,
    *,
    scale,
):
    step = pl.program_id(0)
    coord_dev = grad_ref.shape[1]
    half = own_ref.shape[1]
    core = lax.axis_index("c")

    def pick():
        first = pl.multiple_of(lax.axis_index(CHIPS) * BLOCK, BLOCK)
        part = target_ref.at[:, core, :, pl.ds(first, BLOCK)]
        return pltpu.make_async_copy(part, picked_ref, sems.at[1])

    @pl.when(step == 0)
    def _():
        copy = pltpu.make_async_copy(grad_ref, landed_ref, sems.at[0])
        copy.start()
        pick().start()
        coord = lax.axis_index(PARAM) * coord_dev + lax.broadcasted_iota(
            jnp.int32, mixed_rows_ref.shape, 1
        )
        mixed_rows_ref[...] = fold13(coord * ROW_MUL)
        copy.wait()
        held_ref[...] = landed_ref[...].T

    feat = step * FEAT_TILE + lax.broadcasted_iota(jnp.int32, (FEAT_TILE, 128), 0)
    mixed_feat = fold13(feat * COL_MUL ^ seed_ref[0] * SEED_MUL) ^ TOP_BIT
    tiles = []
    for lane in range(0, coord_dev, 128):
        mixed_coord = jnp.broadcast_to(mixed_rows_ref[0:1, lane : lane + 128], mixed_feat.shape)
        mixed = (mixed_coord ^ mixed_feat) * MIX_MUL
        centred = (mixed ^ jnp.left_shift(mixed, 16)) & HIGH_HALF
        tiles.append(centred.astype(jnp.float32))
    total = lax.dot_general(
        jnp.concatenate(tiles, 1),
        held_ref[...],
        (((1,), (0,)), ((), ())),
        preferred_element_type=jnp.float32,
    ) * (scale * 2.0**-31)
    block = step * (FEAT_TILE // BLOCK)
    for j in range(FEAT_TILE // BLOCK):
        lower = total[j * BLOCK : j * BLOCK + half]
        upper = total[j * BLOCK + half : (j + 1) * BLOCK]

        @pl.when(core == 0)
        def _():
            own_ref[block + j] = lower
            send_ref[block + j] = upper.astype(send_ref.dtype)

        @pl.when(core == 1)
        def _():
            own_ref[block + j] = upper
            send_ref[block + j] = lower.astype(send_ref.dtype)

    @pl.when(step == pl.num_programs(0) - 1)
    def _():
        pick().wait()


def project(gradients, projection_seed, targets):
    chips, _, rows, _ = targets.shape
    exam_dev, coord_dev = gradients.shape
    total_coords = coord_dev * lax.axis_size(PARAM)
    blocks = FEATS // BLOCK
    own = jax.ShapeDtypeStruct((blocks, BLOCK // 2, exam_dev), jnp.float32)
    send = jax.ShapeDtypeStruct(own.shape, jnp.bfloat16)
    vmem = pl.BlockSpec(memory_space=pltpu.VMEM)
    return pl.pallas_call(
        functools.partial(project_kernel, scale=math.sqrt(3.0 / total_coords)),
        out_shape=[own, send, jax.ShapeDtypeStruct((chips, rows, BLOCK), targets.dtype)],
        grid_spec=pltpu.PrefetchScalarGridSpec(
            num_scalar_prefetch=1,
            grid=(FEATS // FEAT_TILE,),
            in_specs=[pl.BlockSpec(memory_space=pl.ANY)] * 2,
            out_specs=[vmem] * 3,
            scratch_shapes=[
                pltpu.VMEM((8, coord_dev), jnp.int32),
                pltpu.VMEM((exam_dev, coord_dev), gradients.dtype),
                pltpu.VMEM((coord_dev, exam_dev), gradients.dtype),
                pltpu.SemaphoreType.DMA((2,)),
            ],
        ),
        compiler_params=pltpu.CompilerParams(
            dimension_semantics=("arbitrary",), vmem_limit_bytes=52 * 2**20
        ),
        name="project",
    )(projection_seed, gradients, targets)


def split_bf16(value):
    high = value.astype(jnp.bfloat16)
    return high, (value - high.astype(jnp.float32)).astype(jnp.bfloat16)


def dot_split(a, b):
    a_high, a_low = split_bf16(a)
    b_high, b_low = split_bf16(b)
    rows = a.shape[0]
    tall = jnp.dot(
        jnp.concatenate([a_high, a_low], 0), b_high, preferred_element_type=jnp.float32
    )
    return tall[:rows] + (
        tall[rows:] + jnp.dot(a_high, b_low, preferred_element_type=jnp.float32)
    )


def score_kernel(mine_ref, beside_ref, across_ref, far_ref, picked_ref, out_ref):
    core = lax.axis_index("c")

    def features(ref):
        return jnp.concatenate([ref[core], ref[1 - core]], 0)

    mine = features(mine_ref)
    feats = jnp.concatenate(
        [mine, features(beside_ref), features(across_ref), features(far_ref)], 1
    )
    width, examples = feats.shape
    fisher = lax.dot_general(
        feats, feats, (((1,), (1,)), ((), ())), preferred_element_type=jnp.float32
    ) / examples
    row = lax.broadcasted_iota(jnp.int32, (width, width), 0)
    col = lax.broadcasted_iota(jnp.int32, (width, width), 1)
    identity = (row == col).astype(jnp.float32)
    trace_value = jnp.sum(fisher * identity)
    damped = fisher + (DAMPING * trace_value) * identity
    total = jnp.sum(damped * identity)
    iterate = identity / total
    product = damped / total
    for step in range(STEPS):
        if step < STEPS - 1:
            both = jnp.concatenate([iterate, product], 0)
            both = 2.0 * both - dot_split(both, product)
            iterate, product = both[:width], both[width:]
        else:
            iterate = 2.0 * iterate - dot_split(iterate, product)
    inverse_bf = iterate.astype(jnp.bfloat16)
    conditioned = lax.dot_general(
        inverse_bf, mine, (((0,), (0,)), ((), ())), preferred_element_type=jnp.float32
    ).astype(jnp.bfloat16)
    picked = picked_ref[...].reshape(-1, width)
    partial = jnp.dot(picked, conditioned, preferred_element_type=jnp.float32)
    out_ref[...] = partial.reshape(out_ref.shape).astype(out_ref.dtype)


def partial_scores(mine, others, picked):
    chips, rows, _ = picked.shape
    vmem = pl.BlockSpec(memory_space=pltpu.VMEM)
    return pl.pallas_call(
        score_kernel,
        out_shape=jax.ShapeDtypeStruct((chips, rows, mine.shape[2]), jnp.bfloat16),
        in_specs=[vmem] * 5,
        out_specs=vmem,
        compiler_params=pltpu.CompilerParams(vmem_limit_bytes=8 * 2**20),
        name="scores",
    )(mine, *others, picked)


def exchange(array, axis, distance):
    return lax.ppermute(array, axis, [(i, i ^ distance) for i in range(lax.axis_size(axis))])


def spread(array, axes):
    return lax.all_to_all(array, axes, split_axis=0, concat_axis=0, tiled=True)


def on_device(gradients, projection_seed, target_features):
    chips = lax.axis_size(CHIPS)
    rows = target_features.shape[0] // (2 * chips)
    targets = target_features.reshape(chips, 2, rows, FEATS)
    own, send, picked = project(gradients, projection_seed, targets)
    chip_sum = (own + exchange(send, "c", 1)).astype(jnp.bfloat16)
    pieces = spread(chip_sum, CHIPS)
    feats = jnp.sum(pieces.astype(jnp.float32), 0).astype(jnp.bfloat16)
    mine = jnp.stack([feats, exchange(feats, "c", 1)])
    others = [exchange(mine, "y", distance) for distance in (1, 3, 2)]
    partial = partial_scores(mine, others, picked)
    return jnp.sum(spread(partial, CHIPS).astype(jnp.float32), 0)


def solution(mesh):
    z, x, c, y = 8, 4, 2, mesh.shape["ex"]
    assert z * x * c == mesh.shape["param"]
    inner = Mesh(mesh.devices.reshape(z, x, c, y), (*PARAM, "y"))
    return jax.shard_map(
        on_device,
        mesh=inner,
        in_specs=(P("y", PARAM), P(), P()),
        out_specs=P(PARAM, "y"),
        check_vma=False,
    )
```

```python
import functools
import math

import jax
import jax.numpy as jnp
from jax import lax
from jax.experimental import pallas as pl
from jax.experimental.pallas import tpu as pltpu
from jax.sharding import Mesh
from jax.sharding import PartitionSpec as P

PARAM = ("z", "x", "c")
CHIPS = ("z", "x")

FEATS = 4096
BLOCK = 128
STEPS = 10
DAMPING = 0.001

ROW_MUL = 73856093
COL_MUL = 19349663
SEED_MUL = 83492791
MIX_MUL = 1274126177
TOP_BIT = -(2**31)
HIGH_HALF = -65536

FEAT_TILE = 512
LANDINGS = (512, 1536, 6144)


def fold13(value):
    return value ^ jnp.right_shift(value, 13)


def project_kernel(
    seed_ref,
    grad_ref,
    target_ref,
    own_ref,
    send_ref,
    picked_ref,
    mixed_rows_ref,
    held_ref,
    sems,
    *,
    scale,
):
    step = pl.program_id(0)
    coord_dev = grad_ref.shape[1]
    half = own_ref.shape[1]
    core = lax.axis_index("c")

    def pick():
        first = pl.multiple_of(lax.axis_index(CHIPS) * BLOCK, BLOCK)
        part = target_ref.at[:, core, :, pl.ds(first, BLOCK)]
        return pltpu.make_async_copy(part, picked_ref, sems.at[0])

    def land(k):
        part = pl.ds(sum(LANDINGS[:k]), LANDINGS[k])
        return pltpu.make_async_copy(grad_ref.at[:, part], held_ref.at[:, part], sems.at[k + 1])

    @pl.when(step == 0)
    def _():
        for k in range(len(LANDINGS)):
            land(k).start()
        pick().start()
        coord = lax.axis_index(PARAM) * coord_dev + lax.broadcasted_iota(
            jnp.int32, mixed_rows_ref.shape, 1
        )
        mixed_rows_ref[...] = fold13(coord * ROW_MUL)

    feat = step * FEAT_TILE + lax.broadcasted_iota(jnp.int32, (FEAT_TILE, 128), 0)
    mixed_feat = fold13(feat * COL_MUL ^ seed_ref[0] * SEED_MUL) ^ TOP_BIT

    def product(first, count):
        tiles = []
        for lane in range(first, first + count, 128):
            mixed_coord = jnp.broadcast_to(mixed_rows_ref[0:1, lane : lane + 128], mixed_feat.shape)
            mixed = (mixed_coord ^ mixed_feat) * MIX_MUL
            centred = (mixed ^ jnp.left_shift(mixed, 16)) & HIGH_HALF
            tiles.append(centred.astype(jnp.float32))
        return lax.dot_general(
            jnp.concatenate(tiles, 1),
            held_ref[:, first : first + count],
            (((1,), (1,)), ((), ())),
            preferred_element_type=jnp.float32,
        )

    def store(total):
        total = total * (scale * 2.0**-31)
        block = step * (FEAT_TILE // BLOCK)
        for j in range(FEAT_TILE // BLOCK):
            lower = total[j * BLOCK : j * BLOCK + half]
            upper = total[j * BLOCK + half : (j + 1) * BLOCK]

            @pl.when(core == 0)
            def _():
                own_ref[block + j] = lower
                send_ref[block + j] = upper.astype(send_ref.dtype)

            @pl.when(core == 1)
            def _():
                own_ref[block + j] = upper
                send_ref[block + j] = lower.astype(send_ref.dtype)

    @pl.when(step == 0)
    def _():
        total = None
        for k, count in enumerate(LANDINGS):
            land(k).wait()
            part = product(sum(LANDINGS[:k]), count)
            total = part if total is None else total + part
        store(total)

    @pl.when(step > 0)
    def _():
        store(product(0, coord_dev))

    @pl.when(step == pl.num_programs(0) - 1)
    def _():
        pick().wait()


def project(gradients, projection_seed, targets):
    chips, _, rows, _ = targets.shape
    exam_dev, coord_dev = gradients.shape
    assert sum(LANDINGS) == coord_dev
    total_coords = coord_dev * lax.axis_size(PARAM)
    blocks = FEATS // BLOCK
    own = jax.ShapeDtypeStruct((blocks, BLOCK // 2, exam_dev), jnp.float32)
    send = jax.ShapeDtypeStruct(own.shape, jnp.bfloat16)
    vmem = pl.BlockSpec(memory_space=pltpu.VMEM)
    return pl.pallas_call(
        functools.partial(project_kernel, scale=math.sqrt(3.0 / total_coords)),
        out_shape=[own, send, jax.ShapeDtypeStruct((chips, rows, BLOCK), targets.dtype)],
        grid_spec=pltpu.PrefetchScalarGridSpec(
            num_scalar_prefetch=1,
            grid=(FEATS // FEAT_TILE,),
            in_specs=[pl.BlockSpec(memory_space=pl.ANY)] * 2,
            out_specs=[vmem] * 3,
            scratch_shapes=[
                pltpu.VMEM((8, coord_dev), jnp.int32),
                pltpu.VMEM((exam_dev, coord_dev), gradients.dtype),
                pltpu.SemaphoreType.DMA((1 + len(LANDINGS),)),
            ],
        ),
        compiler_params=pltpu.CompilerParams(
            dimension_semantics=("arbitrary",), vmem_limit_bytes=52 * 2**20
        ),
        name="project",
    )(projection_seed, gradients, targets)


def split_bf16(value):
    high = value.astype(jnp.bfloat16)
    return high, (value - high.astype(jnp.float32)).astype(jnp.bfloat16)


def dot_split(a, b):
    a_high, a_low = split_bf16(a)
    b_high, b_low = split_bf16(b)
    rows = a.shape[0]
    tall = jnp.dot(
        jnp.concatenate([a_high, a_low], 0), b_high, preferred_element_type=jnp.float32
    )
    return tall[:rows] + (
        tall[rows:] + jnp.dot(a_high, b_low, preferred_element_type=jnp.float32)
    )


def score_kernel(*refs):
    *half_refs, picked_ref, out_ref = refs
    core = lax.axis_index("c")

    def features(here_ref, there_ref):
        here, there = here_ref[...], there_ref[...]
        return jnp.where(
            core == 0, jnp.concatenate([here, there], 0), jnp.concatenate([there, here], 0)
        )

    every = [features(*half_refs[i : i + 2]) for i in range(0, len(half_refs), 2)]
    mine = every[0]
    feats = jnp.concatenate(every, 1)
    width, examples = feats.shape
    fisher = lax.dot_general(
        feats, feats, (((1,), (1,)), ((), ())), preferred_element_type=jnp.float32
    ) / examples
    row = lax.broadcasted_iota(jnp.int32, (width, width), 0)
    col = lax.broadcasted_iota(jnp.int32, (width, width), 1)
    identity = (row == col).astype(jnp.float32)
    trace_value = jnp.sum(fisher * identity)
    damped = fisher + (DAMPING * trace_value) * identity
    total = jnp.sum(damped * identity)
    iterate = identity / total
    product = damped / total
    for step in range(STEPS):
        if step < STEPS - 1:
            both = jnp.concatenate([iterate, product], 0)
            both = 2.0 * both - dot_split(both, product)
            iterate, product = both[:width], both[width:]
        else:
            iterate = 2.0 * iterate - dot_split(iterate, product)
    inverse_bf = iterate.astype(jnp.bfloat16)
    conditioned = lax.dot_general(
        inverse_bf, mine, (((0,), (0,)), ((), ())), preferred_element_type=jnp.float32
    ).astype(jnp.bfloat16)
    picked = picked_ref[...].reshape(-1, width)
    partial = jnp.dot(picked, conditioned, preferred_element_type=jnp.float32)
    out_ref[...] = partial.reshape(out_ref.shape).astype(out_ref.dtype)


def partial_scores(halves, picked):
    chips, rows, _ = picked.shape
    vmem = pl.BlockSpec(memory_space=pltpu.VMEM)
    return pl.pallas_call(
        score_kernel,
        out_shape=jax.ShapeDtypeStruct((chips, rows, halves[0].shape[1]), jnp.bfloat16),
        in_specs=[vmem] * (len(halves) + 1),
        out_specs=vmem,
        compiler_params=pltpu.CompilerParams(vmem_limit_bytes=8 * 2**20),
        name="scores",
    )(*halves, picked)


def exchange(array, axis, distance):
    return lax.ppermute(array, axis, [(i, i ^ distance) for i in range(lax.axis_size(axis))])


def spread(array, axes):
    return lax.all_to_all(array, axes, split_axis=0, concat_axis=0, tiled=True)


def on_device(gradients, projection_seed, target_features):
    chips = lax.axis_size(CHIPS)
    rows = target_features.shape[0] // (2 * chips)
    targets = target_features.reshape(chips, 2, rows, FEATS)
    own, send, picked = project(gradients, projection_seed, targets)
    chip_sum = (own + exchange(send, "c", 1)).astype(jnp.bfloat16)
    pieces = spread(chip_sum, CHIPS)
    feats = jnp.sum(pieces.astype(jnp.float32), 0).astype(jnp.bfloat16)
    halves = []
    for distance in range(lax.axis_size("y")):
        here = exchange(feats, "y", distance) if distance else feats
        halves += [here, exchange(here, "c", 1)]
    partial = partial_scores(halves, picked)
    return jnp.sum(spread(partial, CHIPS).astype(jnp.float32), 0)


def solution(mesh):
    z, x, c, y = 8, 4, 2, mesh.shape["ex"]
    assert z * x * c == mesh.shape["param"]
    inner = Mesh(mesh.devices.reshape(z, x, c, y), (*PARAM, "y"))
    return jax.shard_map(
        on_device,
        mesh=inner,
        in_specs=(P("y", PARAM), P(), P()),
        out_specs=P(PARAM, "y"),
        check_vma=False,
    )
```

```python
import functools
import math

import jax
import jax.numpy as jnp
from jax import lax
from jax.experimental import pallas as pl
from jax.experimental.pallas import tpu as pltpu
from jax.sharding import Mesh
from jax.sharding import PartitionSpec as P

PARAM = ("z", "x", "c")
CHIPS = ("z", "x")

FEATS = 4096
BLOCK = 128
STEPS = 10
DAMPING = 0.001

ROW_MUL = 73856093
COL_MUL = 19349663
SEED_MUL = 83492791
MIX_MUL = 1274126177
TOP_BIT = -(2**31)
HIGH_HALF = -65536

FEAT_TILE = 512


def fold13(value):
    return value ^ jnp.right_shift(value, 13)


def project_kernel(
    seed_ref,
    grad_ref,
    target_ref,
    own_ref,
    send_ref,
    picked_ref,
    mixed_rows_ref,
    landed_ref,
    held_ref,
    total_ref,
    sems,
    *,
    scale,
):
    step = pl.program_id(0)
    coord_dev = grad_ref.shape[1]
    half = own_ref.shape[1]
    core = lax.axis_index("c")

    def pick():
        first = pl.multiple_of(lax.axis_index(CHIPS) * BLOCK, BLOCK)
        part = target_ref.at[:, core, :, pl.ds(first, BLOCK)]
        return pltpu.make_async_copy(part, picked_ref, sems.at[1])

    @pl.when(step == 0)
    def _():
        copy = pltpu.make_async_copy(grad_ref, landed_ref, sems.at[0])
        copy.start()
        pick().start()
        coord = lax.axis_index(PARAM) * coord_dev + lax.broadcasted_iota(
            jnp.int32, mixed_rows_ref.shape, 1
        )
        mixed_rows_ref[...] = fold13(coord * ROW_MUL)
        copy.wait()
        held_ref[...] = landed_ref[...].T

    feat = step * FEAT_TILE + lax.broadcasted_iota(jnp.int32, (FEAT_TILE, 128), 0)
    mixed_feat = fold13(feat * COL_MUL ^ seed_ref[0] * SEED_MUL) ^ TOP_BIT
    mixed_feat = mixed_feat.reshape(FEAT_TILE // 8, 8, 128)
    tiles = []
    for lane in range(0, coord_dev, 128):
        mixed_coord = mixed_rows_ref[:, lane : lane + 128]
        mixed = (mixed_coord ^ mixed_feat) * MIX_MUL
        centred = (mixed ^ jnp.left_shift(mixed, 16)) & HIGH_HALF
        tiles.append(centred.astype(jnp.float32).reshape(FEAT_TILE, 128))
    total = lax.dot_general(
        jnp.concatenate(tiles, 1),
        held_ref[...],
        (((1,), (0,)), ((), ())),
        preferred_element_type=jnp.float32,
    ) * (scale * 2.0**-31)
    total_ref[...] = total.reshape(total_ref.shape)
    block = step * (FEAT_TILE // BLOCK)
    for j in range(FEAT_TILE // BLOCK):
        own_ref[block + j] = total_ref[2 * j + core]
        send_ref[block + j] = total_ref[2 * j + 1 - core].astype(send_ref.dtype)

    @pl.when(step == pl.num_programs(0) - 1)
    def _():
        pick().wait()


def project(gradients, projection_seed, targets):
    chips, _, rows, _ = targets.shape
    exam_dev, coord_dev = gradients.shape
    total_coords = coord_dev * lax.axis_size(PARAM)
    blocks = FEATS // BLOCK
    own = jax.ShapeDtypeStruct((blocks, BLOCK // 2, exam_dev), jnp.float32)
    send = jax.ShapeDtypeStruct(own.shape, jnp.bfloat16)
    vmem = pl.BlockSpec(memory_space=pltpu.VMEM)
    return pl.pallas_call(
        functools.partial(project_kernel, scale=math.sqrt(3.0 / total_coords)),
        out_shape=[own, send, jax.ShapeDtypeStruct((chips, rows, BLOCK), targets.dtype)],
        grid_spec=pltpu.PrefetchScalarGridSpec(
            num_scalar_prefetch=1,
            grid=(FEATS // FEAT_TILE,),
            in_specs=[pl.BlockSpec(memory_space=pl.ANY)] * 2,
            out_specs=[vmem] * 3,
            scratch_shapes=[
                pltpu.VMEM((8, coord_dev), jnp.int32),
                pltpu.VMEM((exam_dev, coord_dev), gradients.dtype),
                pltpu.VMEM((coord_dev, exam_dev), gradients.dtype),
                pltpu.VMEM((2 * FEAT_TILE // BLOCK, BLOCK // 2, exam_dev), jnp.float32),
                pltpu.SemaphoreType.DMA((2,)),
            ],
        ),
        compiler_params=pltpu.CompilerParams(
            dimension_semantics=("arbitrary",), vmem_limit_bytes=52 * 2**20
        ),
        name="project",
    )(projection_seed, gradients, targets)


def split_bf16(value):
    high = value.astype(jnp.bfloat16)
    return high, (value - high.astype(jnp.float32)).astype(jnp.bfloat16)


def dot_split(a, b):
    a_high, a_low = split_bf16(a)
    b_high, b_low = split_bf16(b)
    rows = a.shape[0]
    tall = jnp.dot(
        jnp.concatenate([a_high, a_low], 0), b_high, preferred_element_type=jnp.float32
    )
    return tall[:rows] + (
        tall[rows:] + jnp.dot(a_high, b_low, preferred_element_type=jnp.float32)
    )


def score_kernel(mine_ref, beside_ref, across_ref, far_ref, picked_ref, out_ref):
    core = lax.axis_index("c")

    def features(ref):
        return jnp.concatenate([ref[core], ref[1 - core]], 0)

    mine = features(mine_ref)
    feats = jnp.concatenate(
        [mine, features(beside_ref), features(across_ref), features(far_ref)], 1
    )
    width, examples = feats.shape
    fisher = lax.dot_general(
        feats, feats, (((1,), (1,)), ((), ())), preferred_element_type=jnp.float32
    ) / examples
    row = lax.broadcasted_iota(jnp.int32, (width, width), 0)
    col = lax.broadcasted_iota(jnp.int32, (width, width), 1)
    identity = (row == col).astype(jnp.float32)
    trace_value = jnp.sum(fisher * identity)
    damped = fisher + (DAMPING * trace_value) * identity
    total = jnp.sum(damped * identity)
    iterate = identity / total
    product = damped / total
    for step in range(STEPS):
        if step < STEPS - 1:
            both = jnp.concatenate([iterate, product], 0)
            both = 2.0 * both - dot_split(both, product)
            iterate, product = both[:width], both[width:]
        else:
            iterate = 2.0 * iterate - dot_split(iterate, product)
    inverse_bf = iterate.astype(jnp.bfloat16)
    conditioned = lax.dot_general(
        inverse_bf, mine, (((0,), (0,)), ((), ())), preferred_element_type=jnp.float32
    ).astype(jnp.bfloat16)
    picked = picked_ref[...].reshape(-1, width)
    partial = jnp.dot(picked, conditioned, preferred_element_type=jnp.float32)
    out_ref[...] = partial.reshape(out_ref.shape).astype(out_ref.dtype)


def partial_scores(mine, others, picked):
    chips, rows, _ = picked.shape
    vmem = pl.BlockSpec(memory_space=pltpu.VMEM)
    return pl.pallas_call(
        score_kernel,
        out_shape=jax.ShapeDtypeStruct((chips, rows, mine.shape[2]), jnp.bfloat16),
        in_specs=[vmem] * 5,
        out_specs=vmem,
        compiler_params=pltpu.CompilerParams(
            vmem_limit_bytes=8 * 2**20
        ),
        name="scores",
    )(mine, *others, picked)


def exchange(array, axis, distance):
    return lax.ppermute(array, axis, [(i, i ^ distance) for i in range(lax.axis_size(axis))])


def spread(array, axes):
    return lax.all_to_all(array, axes, split_axis=0, concat_axis=0, tiled=True)


def on_device(gradients, projection_seed, target_features):
    chips = lax.axis_size(CHIPS)
    rows = target_features.shape[0] // (2 * chips)
    targets = target_features.reshape(chips, 2, rows, FEATS)
    own, send, picked = project(gradients, projection_seed, targets)
    chip_sum = (own + exchange(send, "c", 1)).astype(jnp.bfloat16)
    pieces = spread(chip_sum, CHIPS)
    feats = jnp.sum(pieces.astype(jnp.float32), 0).astype(jnp.bfloat16)
    mine = jnp.stack([feats, exchange(feats, "c", 1)])
    others = [exchange(mine, "y", distance) for distance in (1, 3, 2)]
    partial = partial_scores(mine, others, picked)
    return jnp.sum(spread(partial, CHIPS).astype(jnp.float32), 0)


def solution(mesh):
    z, x, c, y = 8, 4, 2, mesh.shape["ex"]
    assert z * x * c == mesh.shape["param"]
    inner = Mesh(mesh.devices.reshape(z, x, c, y), (*PARAM, "y"))
    return jax.shard_map(
        on_device,
        mesh=inner,
        in_specs=(P("y", PARAM), P(), P()),
        out_specs=P(PARAM, "y"),
        check_vma=False,
    )
```

```python
import functools
import math

import jax
import jax.numpy as jnp
from jax import lax
from jax.experimental import pallas as pl
from jax.experimental.pallas import tpu as pltpu
from jax.sharding import Mesh
from jax.sharding import PartitionSpec as P

PARAM = ("z", "x", "c")
CHIPS = ("z", "x")

FEATS = 4096
BLOCK = 128
STEPS = 10
DAMPING = 0.001

ROW_MUL = 73856093
COL_MUL = 19349663
SEED_MUL = 83492791
MIX_MUL = 1274126177
TOP_BIT = -(2**31)
HIGH_HALF = -65536

FEAT_TILE = 1024
LANDING = 1024


def fold13(value):
    return value ^ jnp.right_shift(value, 13)


def project_kernel(
    seed_ref,
    grad_ref,
    target_ref,
    own_ref,
    send_ref,
    picked_ref,
    mixed_rows_ref,
    landed_ref,
    held_ref,
    total_ref,
    sems,
    *,
    scale,
):
    step = pl.program_id(0)
    coord_dev = grad_ref.shape[1]
    half = own_ref.shape[1]
    core = lax.axis_index("c")

    def pick():
        first = pl.multiple_of(lax.axis_index(CHIPS) * BLOCK, BLOCK)
        part = target_ref.at[:, core, :, pl.ds(first, BLOCK)]
        return pltpu.make_async_copy(part, picked_ref, sems.at[0])

    def land(k):
        part = pl.ds(k * LANDING, LANDING)
        return pltpu.make_async_copy(grad_ref.at[:, part], landed_ref.at[:, part], sems.at[k + 1])

    @pl.when(step == 0)
    def _():
        for k in range(coord_dev // LANDING):
            land(k).start()
        pick().start()
        coord = lax.axis_index(PARAM) * coord_dev + lax.broadcasted_iota(
            jnp.int32, mixed_rows_ref.shape, 1
        )
        mixed_rows_ref[...] = fold13(coord * ROW_MUL)
        for k in range(coord_dev // LANDING):
            land(k).wait()
            part = slice(k * LANDING, (k + 1) * LANDING)
            held_ref[part, :] = landed_ref[:, part].T

    feat = step * FEAT_TILE + lax.broadcasted_iota(jnp.int32, (FEAT_TILE, 128), 0)
    mixed_feat = fold13(feat * COL_MUL ^ seed_ref[0] * SEED_MUL) ^ TOP_BIT
    mixed_feat = mixed_feat.reshape(FEAT_TILE // 8, 8, 128)
    tiles = []
    for lane in range(0, coord_dev, 128):
        mixed_coord = mixed_rows_ref[:, lane : lane + 128]
        mixed = (mixed_coord ^ mixed_feat) * MIX_MUL
        centred = (mixed ^ jnp.left_shift(mixed, 16)) & HIGH_HALF
        tiles.append(centred.astype(jnp.float32).reshape(FEAT_TILE, 128))
    total = lax.dot_general(
        jnp.concatenate(tiles, 1),
        held_ref[...],
        (((1,), (0,)), ((), ())),
        preferred_element_type=jnp.float32,
    ) * (scale * 2.0**-31)
    total_ref[...] = total.reshape(total_ref.shape)
    block = step * (FEAT_TILE // BLOCK)
    for j in range(FEAT_TILE // BLOCK):
        own_ref[block + j] = total_ref[2 * j + core]
        send_ref[block + j] = total_ref[2 * j + 1 - core].astype(send_ref.dtype)

    @pl.when(step == pl.num_programs(0) - 1)
    def _():
        pick().wait()


def project(gradients, projection_seed, targets):
    chips, _, rows, _ = targets.shape
    exam_dev, coord_dev = gradients.shape
    total_coords = coord_dev * lax.axis_size(PARAM)
    blocks = FEATS // BLOCK
    own = jax.ShapeDtypeStruct((blocks, BLOCK // 2, exam_dev), jnp.float32)
    send = jax.ShapeDtypeStruct(own.shape, jnp.bfloat16)
    vmem = pl.BlockSpec(memory_space=pltpu.VMEM)
    return pl.pallas_call(
        functools.partial(project_kernel, scale=math.sqrt(3.0 / total_coords)),
        out_shape=[own, send, jax.ShapeDtypeStruct((chips, rows, BLOCK), targets.dtype)],
        grid_spec=pltpu.PrefetchScalarGridSpec(
            num_scalar_prefetch=1,
            grid=(FEATS // FEAT_TILE,),
            in_specs=[pl.BlockSpec(memory_space=pl.ANY)] * 2,
            out_specs=[vmem] * 3,
            scratch_shapes=[
                pltpu.VMEM((8, coord_dev), jnp.int32),
                pltpu.VMEM((exam_dev, coord_dev), gradients.dtype),
                pltpu.VMEM((coord_dev, exam_dev), gradients.dtype),
                pltpu.VMEM((2 * FEAT_TILE // BLOCK, BLOCK // 2, exam_dev), jnp.float32),
                pltpu.SemaphoreType.DMA((1 + coord_dev // LANDING,)),
            ],
        ),
        compiler_params=pltpu.CompilerParams(
            dimension_semantics=("arbitrary",), vmem_limit_bytes=52 * 2**20
        ),
        name="project",
    )(projection_seed, gradients, targets)


def split_bf16(value):
    high = value.astype(jnp.bfloat16)
    return high, (value - high.astype(jnp.float32)).astype(jnp.bfloat16)


def dot_split(a, b):
    a_high, a_low = split_bf16(a)
    b_high, b_low = split_bf16(b)
    rows = a.shape[0]
    tall = jnp.dot(
        jnp.concatenate([a_high, a_low], 0), b_high, preferred_element_type=jnp.float32
    )
    return tall[:rows] + (
        tall[rows:] + jnp.dot(a_high, b_low, preferred_element_type=jnp.float32)
    )


def score_kernel(mine_ref, beside_ref, across_ref, far_ref, picked_ref, out_ref):
    core = lax.axis_index("c")

    def features(ref):
        return jnp.concatenate([ref[core], ref[1 - core]], 0)

    mine = features(mine_ref)
    feats = jnp.concatenate(
        [mine, features(beside_ref), features(across_ref), features(far_ref)], 1
    )
    width, examples = feats.shape
    fisher = lax.dot_general(
        feats, feats, (((1,), (1,)), ((), ())), preferred_element_type=jnp.float32
    ) / examples
    row = lax.broadcasted_iota(jnp.int32, (width, width), 0)
    col = lax.broadcasted_iota(jnp.int32, (width, width), 1)
    identity = (row == col).astype(jnp.float32)
    trace_value = jnp.sum(fisher * identity)
    damped = fisher + (DAMPING * trace_value) * identity
    total = jnp.sum(damped * identity)
    iterate = identity / total
    product = damped / total
    for step in range(STEPS):
        if step < STEPS - 1:
            both = jnp.concatenate([iterate, product], 0)
            both = 2.0 * both - dot_split(both, product)
            iterate, product = both[:width], both[width:]
        else:
            iterate = 2.0 * iterate - dot_split(iterate, product)
    inverse_bf = iterate.astype(jnp.bfloat16)
    conditioned = lax.dot_general(
        inverse_bf, mine, (((0,), (0,)), ((), ())), preferred_element_type=jnp.float32
    ).astype(jnp.bfloat16)
    picked = picked_ref[...].reshape(-1, width)
    partial = jnp.dot(picked, conditioned, preferred_element_type=jnp.float32)
    out_ref[...] = partial.reshape(out_ref.shape).astype(out_ref.dtype)


def partial_scores(mine, others, picked):
    chips, rows, _ = picked.shape
    vmem = pl.BlockSpec(memory_space=pltpu.VMEM)
    return pl.pallas_call(
        score_kernel,
        out_shape=jax.ShapeDtypeStruct((chips, rows, mine.shape[2]), jnp.bfloat16),
        in_specs=[vmem] * 5,
        out_specs=vmem,
        compiler_params=pltpu.CompilerParams(
            vmem_limit_bytes=8 * 2**20
        ),
        name="scores",
    )(mine, *others, picked)


def exchange(array, axis, distance):
    return lax.ppermute(array, axis, [(i, i ^ distance) for i in range(lax.axis_size(axis))])


def spread(array, axes):
    return lax.all_to_all(array, axes, split_axis=0, concat_axis=0, tiled=True)


def on_device(gradients, projection_seed, target_features):
    chips = lax.axis_size(CHIPS)
    rows = target_features.shape[0] // (2 * chips)
    targets = target_features.reshape(chips, 2, rows, FEATS)
    own, send, picked = project(gradients, projection_seed, targets)
    chip_sum = (own + exchange(send, "c", 1)).astype(jnp.bfloat16)
    pieces = spread(chip_sum, CHIPS)
    feats = jnp.sum(pieces.astype(jnp.float32), 0).astype(jnp.bfloat16)
    mine = jnp.stack([feats, exchange(feats, "c", 1)])
    others = [exchange(mine, "y", distance) for distance in (1, 3, 2)]
    partial = partial_scores(mine, others, picked)
    return jnp.sum(spread(partial, CHIPS).astype(jnp.float32), 0)


def solution(mesh):
    z, x, c, y = 8, 4, 2, mesh.shape["ex"]
    assert z * x * c == mesh.shape["param"]
    inner = Mesh(mesh.devices.reshape(z, x, c, y), (*PARAM, "y"))
    return jax.shard_map(
        on_device,
        mesh=inner,
        in_specs=(P("y", PARAM), P(), P()),
        out_specs=P(PARAM, "y"),
        check_vma=False,
    )
```

```python
import functools
import math

import jax
import jax.numpy as jnp
from jax import lax
from jax.experimental import pallas as pl
from jax.experimental.pallas import tpu as pltpu
from jax.sharding import Mesh
from jax.sharding import PartitionSpec as P

PARAM = ("z", "x", "c")
CHIPS = ("z", "x")

FEATS = 4096
BLOCK = 128
STEPS = 10
DAMPING = 0.001

ROW_MUL = 73856093
COL_MUL = 19349663
SEED_MUL = 83492791
MIX_MUL = 1274126177
TOP_BIT = -(2**31)
HIGH_HALF = -65536

FEAT_TILE = 1024
LANDING = 1024


def fold13(value):
    return value ^ jnp.right_shift(value, 13)


def project_kernel(
    seed_ref,
    grad_ref,
    target_ref,
    own_ref,
    send_ref,
    picked_ref,
    mixed_rows_ref,
    landed_ref,
    held_ref,
    total_ref,
    sems,
    *,
    scale,
):
    step = pl.program_id(0)
    coord_dev = grad_ref.shape[1]
    half = own_ref.shape[1]
    core = lax.axis_index("c")

    def pick():
        first = pl.multiple_of(lax.axis_index(CHIPS) * BLOCK, BLOCK)
        part = target_ref.at[:, core, :, pl.ds(first, BLOCK)]
        return pltpu.make_async_copy(part, picked_ref, sems.at[0])

    def land(k):
        part = pl.ds(k * LANDING, LANDING)
        return pltpu.make_async_copy(grad_ref.at[:, part], landed_ref.at[:, part], sems.at[k + 1])

    @pl.when(step == 0)
    def _():
        for k in range(coord_dev // LANDING):
            land(k).start()
        pick().start()
        coord = lax.axis_index(PARAM) * coord_dev + lax.broadcasted_iota(
            jnp.int32, mixed_rows_ref.shape, 1
        )
        mixed_rows_ref[...] = fold13(coord * ROW_MUL)
        for k in range(coord_dev // LANDING):
            land(k).wait()
            part = slice(k * LANDING, (k + 1) * LANDING)
            held_ref[part, :] = landed_ref[:, part].T

    feat = step * FEAT_TILE + lax.broadcasted_iota(jnp.int32, (FEAT_TILE, 128), 0)
    mixed_feat = fold13(feat * COL_MUL ^ seed_ref[0] * SEED_MUL) ^ TOP_BIT
    mixed_feat = mixed_feat.reshape(FEAT_TILE // 8, 8, 128)
    tiles = []
    for lane in range(0, coord_dev, 128):
        mixed_coord = mixed_rows_ref[:, lane : lane + 128]
        mixed = (mixed_coord ^ mixed_feat) * MIX_MUL
        centred = (mixed ^ jnp.left_shift(mixed, 16)) & HIGH_HALF
        tiles.append(centred.astype(jnp.float32).reshape(FEAT_TILE, 128))
    total = lax.dot_general(
        jnp.concatenate(tiles, 1),
        held_ref[...],
        (((1,), (0,)), ((), ())),
        preferred_element_type=jnp.float32,
    ) * (scale * 2.0**-31)
    total_ref[...] = total.reshape(total_ref.shape)
    block = step * (FEAT_TILE // BLOCK)
    for j in range(FEAT_TILE // BLOCK):
        own_ref[block + j] = total_ref[2 * j + core]
        send_ref[block + j] = total_ref[2 * j + 1 - core].astype(send_ref.dtype)

    @pl.when(step == pl.num_programs(0) - 1)
    def _():
        pick().wait()


def project(gradients, projection_seed, targets):
    chips, _, rows, _ = targets.shape
    exam_dev, coord_dev = gradients.shape
    total_coords = coord_dev * lax.axis_size(PARAM)
    blocks = FEATS // BLOCK
    own = jax.ShapeDtypeStruct((blocks, BLOCK // 2, exam_dev), jnp.float32)
    send = jax.ShapeDtypeStruct(own.shape, jnp.bfloat16)
    vmem = pl.BlockSpec(memory_space=pltpu.VMEM)
    return pl.pallas_call(
        functools.partial(project_kernel, scale=math.sqrt(3.0 / total_coords)),
        out_shape=[own, send, jax.ShapeDtypeStruct((chips, rows, BLOCK), targets.dtype)],
        grid_spec=pltpu.PrefetchScalarGridSpec(
            num_scalar_prefetch=1,
            grid=(FEATS // FEAT_TILE,),
            in_specs=[pl.BlockSpec(memory_space=pl.ANY)] * 2,
            out_specs=[vmem] * 3,
            scratch_shapes=[
                pltpu.VMEM((8, coord_dev), jnp.int32),
                pltpu.VMEM((exam_dev, coord_dev), gradients.dtype),
                pltpu.VMEM((coord_dev, exam_dev), gradients.dtype),
                pltpu.VMEM((2 * FEAT_TILE // BLOCK, BLOCK // 2, exam_dev), jnp.float32),
                pltpu.SemaphoreType.DMA((1 + coord_dev // LANDING,)),
            ],
        ),
        compiler_params=pltpu.CompilerParams(
            dimension_semantics=("arbitrary",), vmem_limit_bytes=52 * 2**20
        ),
        name="project",
    )(projection_seed, gradients, targets)


def split_bf16(value):
    high = value.astype(jnp.bfloat16)
    return high, (value - high.astype(jnp.float32)).astype(jnp.bfloat16)


def dot_split(a, b):
    a_high, a_low = split_bf16(a)
    b_high, b_low = split_bf16(b)
    rows = a.shape[0]
    tall = jnp.dot(
        jnp.concatenate([a_high, a_low], 0), b_high, preferred_element_type=jnp.float32
    )
    return tall[:rows] + (
        tall[rows:] + jnp.dot(a_high, b_low, preferred_element_type=jnp.float32)
    )


def in_order(ref):
    core = lax.axis_index("c")
    return jnp.concatenate([ref[core], ref[1 - core]], 0)


def pair_kernel(mine_ref, beside_ref, out_ref):
    feats = jnp.concatenate([in_order(mine_ref), in_order(beside_ref)], 1)
    out_ref[...] = lax.dot_general(
        feats, feats, (((1,), (1,)), ((), ())), preferred_element_type=jnp.float32
    )


def pair_fisher(mine, beside):
    vmem = pl.BlockSpec(memory_space=pltpu.VMEM)
    return pl.pallas_call(
        pair_kernel,
        out_shape=jax.ShapeDtypeStruct((BLOCK, BLOCK), jnp.float32),
        in_specs=[vmem] * 2,
        out_specs=vmem,
        compiler_params=pltpu.CompilerParams(vmem_limit_bytes=8 * 2**20),
        name="pair",
    )(mine, beside)


def score_kernel(mine_ref, near_ref, far_ref, picked_ref, out_ref, *, examples):
    mine = in_order(mine_ref)
    width = mine.shape[0]
    fisher = (near_ref[...] + far_ref[...]) / examples
    row = lax.broadcasted_iota(jnp.int32, (width, width), 0)
    col = lax.broadcasted_iota(jnp.int32, (width, width), 1)
    identity = (row == col).astype(jnp.float32)
    trace_value = jnp.sum(fisher * identity)
    damped = fisher + (DAMPING * trace_value) * identity
    total = jnp.sum(damped * identity)
    iterate = identity / total
    product = damped / total
    for step in range(STEPS):
        if step < STEPS - 1:
            both = jnp.concatenate([iterate, product], 0)
            both = 2.0 * both - dot_split(both, product)
            iterate, product = both[:width], both[width:]
        else:
            iterate = 2.0 * iterate - dot_split(iterate, product)
    inverse_bf = iterate.astype(jnp.bfloat16)
    conditioned = lax.dot_general(
        inverse_bf, mine, (((0,), (0,)), ((), ())), preferred_element_type=jnp.float32
    ).astype(jnp.bfloat16)
    picked = picked_ref[...].reshape(-1, width)
    partial = jnp.dot(picked, conditioned, preferred_element_type=jnp.float32)
    out_ref[...] = partial.reshape(out_ref.shape).astype(out_ref.dtype)


def partial_scores(mine, near, far, picked):
    chips, rows, _ = picked.shape
    vmem = pl.BlockSpec(memory_space=pltpu.VMEM)
    return pl.pallas_call(
        functools.partial(score_kernel, examples=mine.shape[2] * lax.axis_size("y")),
        out_shape=jax.ShapeDtypeStruct((chips, rows, mine.shape[2]), jnp.bfloat16),
        in_specs=[vmem] * 4,
        out_specs=vmem,
        compiler_params=pltpu.CompilerParams(
            vmem_limit_bytes=8 * 2**20
        ),
        name="scores",
    )(mine, near, far, picked)


def exchange(array, axis, distance):
    return lax.ppermute(array, axis, [(i, i ^ distance) for i in range(lax.axis_size(axis))])


def spread(array, axes):
    return lax.all_to_all(array, axes, split_axis=0, concat_axis=0, tiled=True)


def on_device(gradients, projection_seed, target_features):
    chips = lax.axis_size(CHIPS)
    rows = target_features.shape[0] // (2 * chips)
    targets = target_features.reshape(chips, 2, rows, FEATS)
    own, send, picked = project(gradients, projection_seed, targets)
    chip_sum = (own + exchange(send, "c", 1)).astype(jnp.bfloat16)
    pieces = spread(chip_sum, CHIPS)
    feats = jnp.sum(pieces.astype(jnp.float32), 0).astype(jnp.bfloat16)
    mine = jnp.stack([feats, exchange(feats, "c", 1)])
    near = pair_fisher(mine, exchange(mine, "y", 1))
    partial = partial_scores(mine, near, exchange(near, "y", 3), picked)
    return jnp.sum(spread(partial, CHIPS).astype(jnp.float32), 0)


def solution(mesh):
    z, x, c, y = 8, 4, 2, mesh.shape["ex"]
    assert z * x * c == mesh.shape["param"]
    inner = Mesh(mesh.devices.reshape(z, x, c, y), (*PARAM, "y"))
    return jax.shard_map(
        on_device,
        mesh=inner,
        in_specs=(P("y", PARAM), P(), P()),
        out_specs=P(PARAM, "y"),
        check_vma=False,
    )
```
